32 devices in a mesh: dp: 2 (over x), expert: 16 (over z, y, core).
Axes of the slice: x: 2, y: 2, z: 4, core: 2. Of those that a mesh axis runs over, the one named last changes fastest.
Arguments:
- tokens: bfloat16 [256, 3584], P(('dp', 'expert')), may hold values from -6 to 6
- cotangent: bfloat16 [256, 3584], P(('dp', 'expert')), may hold values from -6 to 6
- routes: int32 [256, 8], P(('dp', 'expert')), may hold values from 0 to 15, all different within a row; in each aligned block of 8 rows (0 to 7, 8 to 15, ...) at most 6 rows name the same one
- gates: bfloat16 [256, 8], P(('dp', 'expert')), may hold values from 0.049804688 to 1
- w_gate: bfloat16 [16, 3584, 2048], P('expert', None, 'dp'), may hold values from -0.09375 to 0.09375
- w_up: bfloat16 [16, 3584, 2048], P('expert', None, 'dp'), may hold values from -0.09375 to 0.09375
- w_down: bfloat16 [16, 2048, 3584], P('expert', 'dp'), may hold values from -0.125 to 0.125
Outputs:
- grad_tokens: bfloat16 [256, 3584], P(('dp', 'expert'))
- grad_gate: bfloat16 [16, 3584, 2048], P('expert', None, 'dp')
- grad_up: bfloat16 [16, 3584, 2048], P('expert', None, 'dp')
- grad_down: bfloat16 [16, 2048, 3584], P('expert', 'dp')
The draws below stay inside these ranges and needn't reach their ends.
Inputs may be any that keep to these rules, and one draw needn't show every extreme that they name: `routes`: each row names 8 different experts; among the rows of one device no expert is named more than 6 times, a bound that some block reaches.
All inputs are finite; a program needn't handle non-finite values.
Results may differ from the reference program's by a relative error of at most 0.01.
Values may be sent and summed in bfloat16 or wider, within the bound.
A program may use at most 128 MiB of HBM per device.

```python
import math
import jax
import jax.numpy as jnp
import numpy as np
from jax import lax

D = 3584
FF = 2048
TOP = 8
TOK_DEV = 8
EXPERTS = 16
CAP = 6
TOKENS = 256
N_DP = 2
N_EXPERT = 16


def block_levels(key, shape, cuts, low, largest):
    def one(dim, shards_of):
        draws = jax.random.uniform(jax.random.fold_in(jax.random.fold_in(key, 6), dim), (shards_of,), jnp.float32, low / len(cuts), largest / len(cuts))
        return jnp.repeat(jnp.exp(draws), shape[dim] // shards_of).reshape((-1,) + (1,) * (len(shape) - dim - 1))

    loudness = one(*cuts[0])
    for cut in cuts[1:]:
        loudness = loudness * one(*cut)
    return loudness


def assign_block(stream_key, own, number, rows, amount, top, limit, lean):
    order = jax.random.permutation(stream_key, amount)
    crowded, usual = load_shares(amount, rows * top, limit, lean, True), load_shares(amount, rows * top, limit, lean, False)
    places = jnp.arange(amount)

    def named(lengths, rotation):
        used = int((lengths > 0).sum())
        fixed = max(1, used // 4)
        shifted = fixed + (places - fixed + rotation * (used - fixed)) % max(1, amount - fixed)
        return jnp.zeros((amount,), jnp.int32).at[order[jnp.where(places < fixed, places, shifted)]].set(jnp.asarray(lengths, jnp.int32))

    lengths = jnp.where(number % 4 == 0, named(crowded, number // 4), named(usual, number - number // 4 - 1))
    mixed = jax.random.permutation(jax.random.fold_in(own, 3), amount)
    source_of, receiver = mixed[0:amount // 2 * 2:2], mixed[1:amount // 2 * 2:2]
    margin = jnp.minimum(lengths[source_of] - 1, limit - lengths[receiver]) // 2
    margin = jnp.where((source_of == order[0]) | (receiver == order[0]) | (lengths[receiver] == 0), 0, jnp.maximum(margin, 0))
    shifted = jax.random.randint(jax.random.fold_in(own, 4), (amount // 2,), 0, 1 << 20) % (margin + 1)
    lengths = lengths.at[source_of].add(-shifted).at[receiver].add(shifted)
    items = jnp.searchsorted(jnp.cumsum(lengths), jnp.arange(rows * top), side="right").astype(jnp.int32)
    listing = items.reshape(top, rows).T
    listing = listing[jax.random.permutation(jax.random.fold_in(own, 1), rows)]
    rotation = jax.random.randint(jax.random.fold_in(own, 2), (rows, 1), 0, top)
    return jnp.take_along_axis(listing, (jnp.arange(top)[None, :] + rotation) % top, axis=1)


def load_shares(amount, total, limit, slope, full):
    weights = [(1 << 20) // math.isqrt(rank ** slope) + 1 for rank in range(1, amount + 1)]
    largest = limit if full else min(limit, max(-(-total // amount), total * weights[0] // sum(weights)))
    least = 1 if total - largest >= amount - 1 else 0
    counts, spare = [largest] + [least] * (amount - 1), total - largest - least * (amount - 1)
    while spare > 0:
        movable = [i for i in range(1, amount) if counts[i] < largest] or [i for i in range(1, amount) if counts[i] < limit]
        pool, budget = sum([weights[i] for i in movable]), spare
        for i in movable:
            extra = min(limit - counts[i], max(1, budget * weights[i] // pool), spare)
            counts[i] = counts[i] + extra
            spare = spare - extra
    return np.array(counts)


def noise(key, dims, spread, reach, split=(), held_as=jnp.bfloat16):
    result = jax.random.normal(key, dims, jnp.float32) * spread
    if len(split) > 0:
        result = block_levels(key, dims, split, -0.22, 0.18) * result
    return jnp.clip(result, min=-reach, max=reach).astype(held_as)


def setup_inputs(seed: int = 0) -> dict:
    streams_of = jax.random.split(jax.random.key(seed), 8)
    tokens = noise(streams_of[0], (TOKENS, D), 1.0, 6.0, ((0, 32),))
    cotangent = noise(streams_of[1], (TOKENS, D), 1.0, 6.0, ((0, 32),))
    routes_keys = jax.random.split(jax.random.fold_in(streams_of[2], 1), TOKENS // TOK_DEV)
    routes_turns = jax.random.permutation(jax.random.fold_in(streams_of[2], 3), TOKENS // TOK_DEV)
    routes = jax.vmap(lambda own, number: assign_block(jax.random.fold_in(streams_of[2], 2), own, number, TOK_DEV, EXPERTS, TOP, CAP, 2))(routes_keys, routes_turns).reshape((TOKENS, TOP))
    gates = jnp.clip(jnp.exp(math.log(1.0) - 2.9996462 * jax.random.uniform(streams_of[3], (TOKENS, TOP), jnp.float32) ** block_levels(streams_of[3], (TOKENS, TOP), ((0, 32),), -0.2, 0.2)), 0.049804688, 1.0).astype(jnp.bfloat16)
    w_gate = noise(streams_of[4], (EXPERTS, D, FF), D ** -0.5, 0.09375, ((0, 16), (2, 2)))
    w_up = noise(streams_of[5], (EXPERTS, D, FF), D ** -0.5, 0.09375, ((0, 16), (2, 2)))
    w_down = noise(streams_of[6], (EXPERTS, FF, D), FF ** -0.5, 0.125, ((0, 16), (1, 2)))
    return dict(tokens=tokens, cotangent=cotangent, routes=routes, gates=gates, w_gate=w_gate, w_up=w_up, w_down=w_down)


def expert_terms(rows_x, rows_dy, gate_rows, gate_mat, up_mat, down_mat):
    gate_pre = jnp.dot(rows_x, gate_mat, preferred_element_type=jnp.float32)
    up_pre = jnp.dot(rows_x, up_mat, preferred_element_type=jnp.float32)
    sigmoid_g = jax.nn.sigmoid(gate_pre)
    activated = gate_pre * sigmoid_g
    gate_scale = gate_rows.astype(jnp.float32)[:, None]
    hidden = (gate_scale * activated * up_pre).astype(jnp.bfloat16)
    returned = gate_scale * jnp.dot(rows_dy, down_mat.T, preferred_element_type=jnp.float32)
    d_gate = (returned * up_pre * sigmoid_g * (1.0 + gate_pre * (1.0 - sigmoid_g))).astype(jnp.bfloat16)
    d_up = (returned * activated).astype(jnp.bfloat16)
    grad_gate = jnp.dot(rows_x.T, d_gate, preferred_element_type=jnp.float32)
    grad_up = jnp.dot(rows_x.T, d_up, preferred_element_type=jnp.float32)
    grad_down = jnp.dot(hidden.T, rows_dy, preferred_element_type=jnp.float32)
    return d_gate, d_up, grad_gate, grad_up, grad_down


def reference(tokens, cotangent, routes, gates, w_gate, w_up, w_down):
    dev_count = N_DP * N_EXPERT
    flat_ids = routes.reshape(dev_count, TOK_DEV * TOP)
    expert_iota = jnp.arange(EXPERTS, dtype=jnp.int32)
    onehot = (flat_ids[:, :, None] == expert_iota[None, None, :]).astype(jnp.int32)
    slot_pos = jnp.sum((jnp.cumsum(onehot, axis=1) - onehot) * onehot, axis=2).astype(jnp.int32)
    source = jnp.arange(dev_count, dtype=jnp.int32)[:, None]
    position = ((flat_ids * dev_count + source) * CAP + slot_pos).reshape(-1).astype(jnp.int32)
    token_of = (jnp.arange(TOKENS * TOP, dtype=jnp.int32) // TOP).astype(jnp.int32)
    slots_all = EXPERTS * dev_count * CAP
    row_table = jnp.full((slots_all,), TOKENS, jnp.int32).at[position].set(token_of)
    gate_table = jnp.zeros((slots_all,), jnp.float32).at[position].set(gates.reshape(-1).astype(jnp.float32))
    padded_x = jnp.concatenate([tokens, jnp.zeros((1, D), tokens.dtype)], axis=0)
    padded_dy = jnp.concatenate([cotangent, jnp.zeros((1, D), cotangent.dtype)], axis=0)

    def one_expert(carried, inputs):
        row_index, gate_rows, gate_mat, up_mat, down_mat = inputs
        rows_x = padded_x[row_index]
        rows_dy = padded_dy[row_index]
        d_gate, d_up, grad_gate, grad_up, grad_down = expert_terms(rows_x, rows_dy, gate_rows, gate_mat, up_mat, down_mat)
        partial_value = jnp.dot(d_gate, gate_mat.T, preferred_element_type=jnp.float32) + jnp.dot(d_up, up_mat.T, preferred_element_type=jnp.float32)
        return carried.at[row_index].add(partial_value), (grad_gate.astype(jnp.bfloat16), grad_up.astype(jnp.bfloat16), grad_down.astype(jnp.bfloat16))

    initial = jnp.zeros((TOKENS + 1, D), jnp.float32)
    total, grads = lax.scan(one_expert, initial, (row_table.reshape(EXPERTS, dev_count * CAP), gate_table.reshape(EXPERTS, dev_count * CAP), w_gate, w_up, w_down))
    return (total[:TOKENS].astype(jnp.bfloat16), grads[0], grads[1], grads[2])
```

```python
import functools

import jax
import jax.numpy as jnp
from jax import lax
from jax.experimental import pallas as pl
from jax.experimental.pallas import tpu as pltpu
from jax.sharding import PartitionSpec as P


def slot_index(flat_ids, expert_count):
    onehot = (flat_ids[..., None] == jnp.arange(expert_count, dtype=jnp.int32)).astype(jnp.int32)
    return jnp.sum((jnp.cumsum(onehot, axis=-2) - onehot) * onehot, axis=-1)


def expert_terms(rows_x, rows_dy, gate_rows, gate_mat, up_mat, down_mat):
    gate_pre = jnp.dot(rows_x, gate_mat, preferred_element_type=jnp.float32)
    up_pre = jnp.dot(rows_x, up_mat, preferred_element_type=jnp.float32)
    sigmoid_g = jax.nn.sigmoid(gate_pre)
    activated = gate_pre * sigmoid_g
    gate_scale = gate_rows.astype(jnp.float32)[:, None]
    hidden = (gate_scale * activated * up_pre).astype(jnp.bfloat16)
    returned = gate_scale * jnp.dot(rows_dy, down_mat.T, preferred_element_type=jnp.float32)
    d_gate = (returned * up_pre * sigmoid_g * (1.0 + gate_pre * (1.0 - sigmoid_g))).astype(
        jnp.bfloat16
    )
    d_up = (returned * activated).astype(jnp.bfloat16)
    grad_gate = jnp.dot(rows_x.T, d_gate, preferred_element_type=jnp.float32)
    grad_up = jnp.dot(rows_x.T, d_up, preferred_element_type=jnp.float32)
    grad_down = jnp.dot(hidden.T, rows_dy, preferred_element_type=jnp.float32)
    return (d_gate, d_up, grad_gate, grad_up, grad_down)


def routed_per_device(tokens, cotangent, routes, gates, w_gate, w_up, w_down):
    tok_rows, features = tokens.shape
    top_k = routes.shape[1]
    expert_count = lax.axis_size("expert")
    capacity = min(tok_rows, (3 * tok_rows * top_k + 2 * expert_count - 1) // (2 * expert_count))
    gate_mat = w_gate[0]
    up_mat = w_up[0]
    down_mat = w_down[0]
    flat_ids = routes.reshape(-1)
    position = flat_ids * capacity + slot_index(flat_ids, expert_count)
    token_of = jnp.arange(tok_rows * top_k, dtype=jnp.int32) // top_k
    slots_all = expert_count * capacity
    send_x = jnp.zeros((slots_all, features), jnp.bfloat16).at[position].set(tokens[token_of])
    send_dy = jnp.zeros((slots_all, features), jnp.bfloat16).at[position].set(cotangent[token_of])
    send_gate = jnp.zeros((slots_all,), jnp.bfloat16).at[position].set(gates.reshape(-1))
    received = (
        lax.all_to_all(
            send_x.reshape(expert_count, capacity, features),
            "expert",
            split_axis=0,
            concat_axis=0,
            tiled=True,
        ),
        lax.all_to_all(
            send_dy.reshape(expert_count, capacity, features),
            "expert",
            split_axis=0,
            concat_axis=0,
            tiled=True,
        ),
        lax.all_to_all(
            send_gate.reshape(expert_count, capacity),
            "expert",
            split_axis=0,
            concat_axis=0,
            tiled=True,
        ),
    )
    gathered = (
        lax.all_gather(received[0], "dp", axis=0, tiled=True),
        lax.all_gather(received[1], "dp", axis=0, tiled=True),
        lax.all_gather(received[2], "dp", axis=0, tiled=True),
    )
    rows_x = gathered[0].reshape(-1, features)
    rows_dy = gathered[1].reshape(-1, features)
    d_gate, d_up, grad_gate, grad_up, grad_down = expert_terms(
        rows_x, rows_dy, gathered[2].reshape(-1), gate_mat, up_mat, down_mat
    )
    own_rows = lax.psum_scatter(
        jnp.dot(d_gate, gate_mat.T, preferred_element_type=jnp.float32)
        + jnp.dot(d_up, up_mat.T, preferred_element_type=jnp.float32),
        "dp",
        scatter_dimension=0,
        tiled=True,
    )
    returned = lax.all_to_all(
        own_rows.reshape(expert_count, capacity, features),
        "expert",
        split_axis=0,
        concat_axis=0,
        tiled=True,
    )
    selected = returned.reshape(slots_all, features)[position]
    grad_x = selected.reshape(tok_rows, top_k, features).sum(axis=1)
    return (
        grad_x.astype(jnp.bfloat16),
        grad_gate.astype(jnp.bfloat16)[None],
        grad_up.astype(jnp.bfloat16)[None],
        grad_down.astype(jnp.bfloat16)[None],
    )


LANES = 128
NT = (((1,), (1,)), ((), ()))


def pick(options, size):
    return next((o for o in options if size % o == 0), size)


def main_kernel(tile, sel_ref, x_ref, dy_ref, coef_ref, wg_ref, wu_ref, wd_ref, p_ref, gg_ref, gu_ref, gd_ref, xt_ref, acc_ref):
    step = pl.program_id(0)
    features = x_ref.shape[1]

    @pl.when(step == 0)
    def _():
        for t in range(0, features, tile):
            xt_ref[t:t + tile, :] = x_ref[:, t:t + tile].T

    c = jnp.sum(coef_ref[...].astype(jnp.float32) * sel_ref[...], axis=1, keepdims=True)
    x = x_ref[...]
    g = jnp.dot(x, wg_ref[...], preferred_element_type=jnp.float32)
    u = jnp.dot(x, wu_ref[...], preferred_element_type=jnp.float32)
    r = c * lax.dot_general(dy_ref[...], wd_ref[...], NT, preferred_element_type=jnp.float32)
    s = jax.nn.sigmoid(g)
    act = g * s
    hid_t = (c * act * u).astype(jnp.bfloat16).T
    dg = (r * u * s * (1.0 + g * (1.0 - s))).astype(jnp.bfloat16)
    du = (r * act).astype(jnp.bfloat16)

    for t in range(0, features, tile):
        cols = slice(t, t + tile)
        part = lax.dot_general(dg, wg_ref[cols, :], NT, preferred_element_type=jnp.float32)
        part += lax.dot_general(du, wu_ref[cols, :], NT, preferred_element_type=jnp.float32)

        @pl.when(step == 0)
        def _():
            acc_ref[:, cols] = part

        @pl.when(step > 0)
        def _():
            acc_ref[:, cols] += part

        gg_ref[cols, :] = jnp.dot(xt_ref[cols, :], dg, preferred_element_type=jnp.float32).astype(jnp.bfloat16)
        gu_ref[cols, :] = jnp.dot(xt_ref[cols, :], du, preferred_element_type=jnp.float32).astype(jnp.bfloat16)
        gd_ref[:, cols] = jnp.dot(hid_t, dy_ref[:, cols], preferred_element_type=jnp.float32).astype(jnp.bfloat16)

    @pl.when(step == pl.num_programs(0) - 1)
    def _():
        p_ref[...] = acc_ref[...].astype(jnp.bfloat16)


def main_call(sel, gathered, w_gate, w_up, w_down):
    _, features, hidden = w_gate.shape
    rows = gathered.shape[0]
    chunk = pick((256, 128), hidden)
    tile = pick((512, 256, 128), features)
    whole = lambda width, index: pl.BlockSpec((rows, width), lambda i: (0, index), pipeline_mode=pl.Buffered(1))
    col = pl.BlockSpec((None, features, chunk), lambda i: (0, 0, i))
    row = pl.BlockSpec((None, chunk, features), lambda i: (0, i, 0))
    bf = jnp.bfloat16
    return pl.pallas_call(
        functools.partial(main_kernel, tile),
        grid=(hidden // chunk,),
        in_specs=[
            pl.BlockSpec((1, LANES), lambda i: (0, 0)),
            whole(features, 0), whole(features, 1), whole(LANES, 2 * features // LANES),
            col, col, row,
        ],
        out_specs=[pl.BlockSpec((rows, features), lambda i: (0, 0)), col, col, row],
        out_shape=[
            jax.ShapeDtypeStruct((rows, features), bf),
            jax.ShapeDtypeStruct(w_gate.shape, bf),
            jax.ShapeDtypeStruct(w_up.shape, bf),
            jax.ShapeDtypeStruct(w_down.shape, bf),
        ],
        scratch_shapes=[pltpu.VMEM((features, rows), bf), pltpu.VMEM((rows, features), jnp.float32)],
        compiler_params=pltpu.CompilerParams(dimension_semantics=("arbitrary",), vmem_limit_bytes=60 << 20),
    )(sel, gathered, gathered, gathered, w_gate, w_up, w_down)


def payload_of(tokens, cotangent, routes, gates):
    lanes = jnp.arange(LANES, dtype=jnp.int32)
    hit = routes[:, :, None] == lanes[None, None, :]
    coef = jnp.sum(jnp.where(hit, gates[:, :, None].astype(jnp.float32), 0.0), axis=1)
    return jnp.concatenate([tokens, cotangent, coef.astype(jnp.bfloat16)], axis=1)


def dense_per_device(tokens, cotangent, routes, gates, w_gate, w_up, w_down):
    payload = payload_of(tokens, cotangent, routes, gates)
    gathered = lax.all_gather(payload, ("dp", "expert"), axis=0, tiled=True)
    sel = (jnp.arange(LANES, dtype=jnp.int32) == lax.axis_index("expert")).astype(jnp.float32)[None]
    partial, grad_gate, grad_up, grad_down = main_call(sel, gathered, w_gate, w_up, w_down)
    grad_x = lax.psum_scatter(partial, ("dp", "expert"), scatter_dimension=0, tiled=True)
    return grad_x, grad_gate, grad_up, grad_down


def per_device(tokens, cotangent, routes, gates, w_gate, w_up, w_down):
    features = tokens.shape[1]
    rows = tokens.shape[0] * lax.axis_size("dp") * lax.axis_size("expert")
    chunk = pick((256, 128), w_gate.shape[2])
    need = features * (14 * rows + 24 * chunk)
    fits = need < (56 << 20) and lax.axis_size("expert") <= LANES and features % LANES == 0
    body = dense_per_device if fits else routed_per_device
    return body(tokens, cotangent, routes, gates, w_gate, w_up, w_down)


def solution(mesh):
    return jax.shard_map(
        per_device,
        mesh=mesh,
        in_specs=(
            P(("dp", "expert"), None),
            P(("dp", "expert"), None),
            P(("dp", "expert"), None),
            P(("dp", "expert"), None),
            P("expert", None, "dp"),
            P("expert", None, "dp"),
            P("expert", "dp", None),
        ),
        out_specs=(
            P(("dp", "expert"), None),
            P("expert", None, "dp"),
            P("expert", None, "dp"),
            P("expert", "dp", None),
        ),
        check_vma=False,
    )
```

```python
import functools
import itertools
import math

import jax
import jax.numpy as jnp
import numpy as np
from jax import lax
from jax.experimental import pallas as pl
from jax.experimental.pallas import tpu as pltpu
from jax.sharding import PartitionSpec as P


def slot_index(flat_ids, expert_count):
    onehot = (flat_ids[..., None] == jnp.arange(expert_count, dtype=jnp.int32)).astype(jnp.int32)
    return jnp.sum((jnp.cumsum(onehot, axis=-2) - onehot) * onehot, axis=-1)


def expert_terms(rows_x, rows_dy, gate_rows, gate_mat, up_mat, down_mat):
    gate_pre = jnp.dot(rows_x, gate_mat, preferred_element_type=jnp.float32)
    up_pre = jnp.dot(rows_x, up_mat, preferred_element_type=jnp.float32)
    sigmoid_g = jax.nn.sigmoid(gate_pre)
    activated = gate_pre * sigmoid_g
    gate_scale = gate_rows.astype(jnp.float32)[:, None]
    hidden = (gate_scale * activated * up_pre).astype(jnp.bfloat16)
    returned = gate_scale * jnp.dot(rows_dy, down_mat.T, preferred_element_type=jnp.float32)
    d_gate = (returned * up_pre * sigmoid_g * (1.0 + gate_pre * (1.0 - sigmoid_g))).astype(
        jnp.bfloat16
    )
    d_up = (returned * activated).astype(jnp.bfloat16)
    grad_gate = jnp.dot(rows_x.T, d_gate, preferred_element_type=jnp.float32)
    grad_up = jnp.dot(rows_x.T, d_up, preferred_element_type=jnp.float32)
    grad_down = jnp.dot(hidden.T, rows_dy, preferred_element_type=jnp.float32)
    return (d_gate, d_up, grad_gate, grad_up, grad_down)


def routed_per_device(tokens, cotangent, routes, gates, w_gate, w_up, w_down):
    tok_rows, features = tokens.shape
    top_k = routes.shape[1]
    expert_count = lax.axis_size("expert")
    capacity = min(tok_rows, (3 * tok_rows * top_k + 2 * expert_count - 1) // (2 * expert_count))
    gate_mat = w_gate[0]
    up_mat = w_up[0]
    down_mat = w_down[0]
    flat_ids = routes.reshape(-1)
    position = flat_ids * capacity + slot_index(flat_ids, expert_count)
    token_of = jnp.arange(tok_rows * top_k, dtype=jnp.int32) // top_k
    slots_all = expert_count * capacity
    send_x = jnp.zeros((slots_all, features), jnp.bfloat16).at[position].set(tokens[token_of])
    send_dy = jnp.zeros((slots_all, features), jnp.bfloat16).at[position].set(cotangent[token_of])
    send_gate = jnp.zeros((slots_all,), jnp.bfloat16).at[position].set(gates.reshape(-1))
    received = (
        lax.all_to_all(
            send_x.reshape(expert_count, capacity, features),
            "expert",
            split_axis=0,
            concat_axis=0,
            tiled=True,
        ),
        lax.all_to_all(
            send_dy.reshape(expert_count, capacity, features),
            "expert",
            split_axis=0,
            concat_axis=0,
            tiled=True,
        ),
        lax.all_to_all(
            send_gate.reshape(expert_count, capacity),
            "expert",
            split_axis=0,
            concat_axis=0,
            tiled=True,
        ),
    )
    gathered = (
        lax.all_gather(received[0], "dp", axis=0, tiled=True),
        lax.all_gather(received[1], "dp", axis=0, tiled=True),
        lax.all_gather(received[2], "dp", axis=0, tiled=True),
    )
    rows_x = gathered[0].reshape(-1, features)
    rows_dy = gathered[1].reshape(-1, features)
    d_gate, d_up, grad_gate, grad_up, grad_down = expert_terms(
        rows_x, rows_dy, gathered[2].reshape(-1), gate_mat, up_mat, down_mat
    )
    own_rows = lax.psum_scatter(
        jnp.dot(d_gate, gate_mat.T, preferred_element_type=jnp.float32)
        + jnp.dot(d_up, up_mat.T, preferred_element_type=jnp.float32),
        "dp",
        scatter_dimension=0,
        tiled=True,
    )
    returned = lax.all_to_all(
        own_rows.reshape(expert_count, capacity, features),
        "expert",
        split_axis=0,
        concat_axis=0,
        tiled=True,
    )
    selected = returned.reshape(slots_all, features)[position]
    grad_x = selected.reshape(tok_rows, top_k, features).sum(axis=1)
    return (
        grad_x.astype(jnp.bfloat16),
        grad_gate.astype(jnp.bfloat16)[None],
        grad_up.astype(jnp.bfloat16)[None],
        grad_down.astype(jnp.bfloat16)[None],
    )


LANES = 128
NT = (((1,), (1,)), ((), ()))


def pick(options, size):
    return next((o for o in options if size % o == 0), size)


def main_kernel(tile, sel_ref, x_ref, dy_ref, coef_ref, wg_ref, wu_ref, wd_ref, p_ref, gg_ref, gu_ref, gd_ref, xt_ref, acc_ref):
    step = pl.program_id(0)
    features = x_ref.shape[1]

    @pl.when(step == 0)
    def _():
        for t in range(0, features, tile):
            xt_ref[t:t + tile, :] = x_ref[:, t:t + tile].T

    c = jnp.sum(coef_ref[...].astype(jnp.float32) * sel_ref[...], axis=1, keepdims=True)
    x = x_ref[...]
    g = jnp.dot(x, wg_ref[...], preferred_element_type=jnp.float32)
    u = jnp.dot(x, wu_ref[...], preferred_element_type=jnp.float32)
    r = c * lax.dot_general(dy_ref[...], wd_ref[...], NT, preferred_element_type=jnp.float32)
    s = jax.nn.sigmoid(g)
    act = g * s
    hid_t = (c * act * u).astype(jnp.bfloat16).T
    dg = (r * u * s * (1.0 + g * (1.0 - s))).astype(jnp.bfloat16)
    du = (r * act).astype(jnp.bfloat16)

    for t in range(0, features, tile):
        cols = slice(t, t + tile)
        part = lax.dot_general(dg, wg_ref[cols, :], NT, preferred_element_type=jnp.float32)
        part += lax.dot_general(du, wu_ref[cols, :], NT, preferred_element_type=jnp.float32)

        @pl.when(step == 0)
        def _():
            acc_ref[:, cols] = part

        @pl.when(step > 0)
        def _():
            acc_ref[:, cols] += part

        gg_ref[cols, :] = jnp.dot(xt_ref[cols, :], dg, preferred_element_type=jnp.float32).astype(jnp.bfloat16)
        gu_ref[cols, :] = jnp.dot(xt_ref[cols, :], du, preferred_element_type=jnp.float32).astype(jnp.bfloat16)
        gd_ref[:, cols] = jnp.dot(hid_t, dy_ref[:, cols], preferred_element_type=jnp.float32).astype(jnp.bfloat16)

    @pl.when(step == pl.num_programs(0) - 1)
    def _():
        p_ref[...] = acc_ref[...].astype(jnp.bfloat16)


def main_call(sel, gathered, w_gate, w_up, w_down):
    _, features, hidden = w_gate.shape
    rows = gathered[0].shape[0]
    chunk = pick((256, 128), hidden)
    tile = pick((512, 256, 128), features)
    whole = lambda width: pl.BlockSpec((rows, width), lambda i: (0, 0), pipeline_mode=pl.Buffered(1))
    col = pl.BlockSpec((None, features, chunk), lambda i: (0, 0, i))
    row = pl.BlockSpec((None, chunk, features), lambda i: (0, i, 0))
    bf = jnp.bfloat16
    return pl.pallas_call(
        functools.partial(main_kernel, tile),
        grid=(hidden // chunk,),
        in_specs=[
            pl.BlockSpec((1, LANES), lambda i: (0, 0)),
            whole(features), whole(features), whole(LANES),
            col, col, row,
        ],
        out_specs=[pl.BlockSpec((rows, features), lambda i: (0, 0)), col, col, row],
        out_shape=[
            jax.ShapeDtypeStruct((rows, features), bf),
            jax.ShapeDtypeStruct(w_gate.shape, bf),
            jax.ShapeDtypeStruct(w_up.shape, bf),
            jax.ShapeDtypeStruct(w_down.shape, bf),
        ],
        scratch_shapes=[pltpu.VMEM((features, rows), bf), pltpu.VMEM((rows, features), jnp.float32)],
        compiler_params=pltpu.CompilerParams(dimension_semantics=("arbitrary",), vmem_limit_bytes=60 << 20),
    )(sel, *gathered, w_gate, w_up, w_down)


def digits_of(mesh):
    digits = {}
    for number, axis in enumerate(mesh.axis_names):
        line = np.moveaxis(mesh.devices, number, 0)
        line = line.reshape(line.shape[0], -1)[:, 0]
        places = [(*d.coords, d.core_on_chip) for d in line]
        stride = 1
        while stride < len(places):
            name = next(i for i in range(4) if places[stride][i] != places[0][i])
            size = len({p[name] for p in places})
            digits[name] = (axis, stride, size)
            stride *= size
    return digits


class Torus:
    def __init__(self, digits, axis_sizes):
        self.digits, self.axis_sizes = digits, axis_sizes
        self.me = {n: (lax.axis_index(a) // s) % k for n, (a, s, k) in digits.items()}

    def at(self, delta):
        place = dict(self.me)
        for name, step in delta.items():
            size = self.digits[name][2]
            place[name] = (self.me[name] + step) % 2 if size == 2 else self.me[name] + step
        return place

    def device(self, place):
        index = {a: 0 for a in self.axis_sizes}
        for name, (axis, stride, _) in self.digits.items():
            index[axis] = index[axis] + place[name] * stride
        return index

    def linear(self, place):
        index, total = self.device(place), 0
        for axis, size in self.axis_sizes.items():
            total = total * size + index[axis]
        return total

    def steps(self, name):
        return (1,) if self.digits[name][2] == 2 else (1, -1)

    def inside(self, name, step):
        size = self.digits[name][2]
        if size == 2 or step == 0:
            return None
        return self.me[name] + step < size if step > 0 else self.me[name] + step >= 0

    def sites(self, order):
        spans = []
        for name in order:
            size = self.digits[name][2]
            spans.append(range(size) if size == 2 else range(1 - size, size))
        return [dict(zip(order, combo)) for combo in itertools.product(*spans)]

    def valid(self, delta):
        found = None
        for name, step in delta.items():
            test = self.inside(name, step)
            if test is not None:
                found = test if found is None else jnp.logical_and(found, test)
        return found

    def children(self, order, delta):
        last = max([i for i, n in enumerate(order) if delta[n]], default=-1)
        found = []
        if last >= 0 and self.digits[order[last]][2] > 2:
            found.append((order[last], -1 if delta[order[last]] > 0 else 1))
        for name in order[last + 1:]:
            found += [(name, step) for step in self.steps(name)]
        return found

    def parent(self, order, delta):
        last = max(i for i, n in enumerate(order) if delta[n])
        return order[last], 1 if delta[order[last]] > 0 else -1

    def barrier(self):
        sem = pltpu.get_barrier_semaphore()
        count = 0
        for name in self.digits:
            for step in self.steps(name):
                test = self.inside(name, step)
                target = self.device(self.at({name: step}))

                def greet(target=target):
                    pl.semaphore_signal(sem, inc=1, device_id=target, device_id_type=pl.DeviceIdType.MESH)

                when(test, greet)
                count = count + (1 if test is None else test.astype(jnp.int32))
        pl.semaphore_wait(sem, count)


def when(test, body):
    if test is None:
        body()
    else:
        pl.when(test)(body)


def distance(delta):
    return sum(abs(v) for v in delta.values())


def lines_and_pairs(digits):
    lines = [n for n in digits if digits[n][2] > 2]
    pairs = [n for n in digits if digits[n][2] == 2 and n != 3]
    core = [3] if 3 in digits else []
    return tuple(lines + pairs + core), tuple(lines + pairs[::-1] + core)


def gather_kernel(digits, axis_sizes, orders, *refs):
    parts = len(orders)
    ins, outs = refs[:parts], refs[parts:2 * parts]
    send_sem, recv_sem, local_sem = refs[2 * parts:]
    torus = Torus(digits, axis_sizes)
    rows = ins[0].shape[0]

    def block(ref, index):
        return ref.at[pl.ds(pl.multiple_of(index * rows, rows), rows)]

    mine = torus.linear(torus.me)
    own = [pltpu.make_async_copy(ins[p], block(outs[p], mine), local_sem.at[p]) for p in range(parts)]
    torus.barrier()
    plan, used = [], [0] * parts
    for p in range(parts):
        for delta in torus.sites(orders[p]):
            plan.append((distance(delta), p, delta))
    plan.sort(key=lambda entry: entry[:2])
    later = []
    for _, p, delta in plan:
        index = torus.linear(torus.at(delta))
        root = distance(delta) == 0
        copies = []
        for name, step in torus.children(orders[p], delta):
            copies.append((torus.inside(name, step), pltpu.make_async_remote_copy(
                src_ref=ins[p] if root else block(outs[p], index),
                dst_ref=block(outs[p], index),
                send_sem=send_sem.at[p, used[p]],
                recv_sem=recv_sem.at[p, index],
                device_id=torus.device(torus.at({name: step})),
                device_id_type=pl.DeviceIdType.MESH,
            )))
            used[p] += 1

        def handle(p=p, index=index, root=root, copies=copies):
            if not root:
                pltpu.make_async_copy(ins[p], block(outs[p], index), recv_sem.at[p, index]).wait()
            for test, copy in copies:
                when(test, copy.start)

        def finish(copies=copies):
            for test, copy in copies:
                when(test, copy.wait_send)

        test = torus.valid(delta)
        when(test, handle)
        later.append((test, finish))
        if root:
            own[p].start()
    for test, finish in later:
        when(test, finish)
    for copy in own:
        copy.wait()


def gather_call(digits, axis_sizes, arrays):
    first, second = lines_and_pairs(digits)
    orders = (first, second) + (first,) * (len(arrays) - 2)
    devices = math.prod(axis_sizes.values())
    count = max(count_sends(digits, order) for order in orders)
    return pl.pallas_call(
        functools.partial(gather_kernel, digits, axis_sizes, orders),
        in_specs=[pl.BlockSpec(memory_space=pl.ANY)] * len(arrays),
        out_specs=[pl.BlockSpec(memory_space=pl.ANY)] * len(arrays),
        out_shape=[jax.ShapeDtypeStruct((devices * a.shape[0], a.shape[1]), a.dtype) for a in arrays],
        scratch_shapes=[
            pltpu.SemaphoreType.DMA((len(arrays), count)),
            pltpu.SemaphoreType.DMA((len(arrays), devices)),
            pltpu.SemaphoreType.DMA((len(arrays),)),
        ],
        compiler_params=pltpu.CompilerParams(collective_id=0, has_side_effects=True),
    )(*arrays)


def count_sends(digits, order):
    shape = Torus.__new__(Torus)
    shape.digits = digits
    return sum(len(shape.children(order, delta)) for delta in shape.sites(order))


def scatter_kernel(digits, axis_sizes, orders, ways, p_ref, out_ref, land, total, total32, send_sem, recv_sem):
    torus = Torus(digits, axis_sizes)
    parts = len(orders)
    width = p_ref.shape[2] // parts
    plan = []
    for p in range(parts):
        for number, delta in enumerate(torus.sites(orders[p])):
            plan.append((len(torus.children(orders[p], delta)), -distance(delta), p, number, delta))
    plan.sort(key=lambda entry: entry[:4])
    torus.barrier()
    later = []
    for _, _, p, number, delta in plan:
        order = orders[p]
        index = torus.linear(torus.at(delta))
        cols = slice(p * width, (p + 1) * width)
        root = distance(delta) == 0
        kids = torus.children(order, delta)
        source = total if kids else p_ref
        copy = None
        if not root:
            name, step = torus.parent(order, delta)
            way = ways.index((name, step if digits[name][2] == 2 else -step))
            copy = pltpu.make_async_remote_copy(
                src_ref=source.at[index, :, cols],
                dst_ref=land.at[way, index, :, cols],
                send_sem=send_sem.at[p, number],
                recv_sem=recv_sem.at[p, way, index],
                device_id=torus.device(torus.at({name: step})),
                device_id_type=pl.DeviceIdType.MESH,
            )

        def handle(p=p, index=index, cols=cols, kids=kids, copy=copy):
            if kids:
                total32[:, cols] = p_ref[index, :, cols].astype(jnp.float32)
                for name, step in kids:
                    way = ways.index((name, step))

                    def add(way=way):
                        here = land.at[way, index, :, cols]
                        pltpu.make_async_copy(here, here, recv_sem.at[p, way, index]).wait()
                        total32[:, cols] += land[way, index, :, cols].astype(jnp.float32)

                    when(torus.inside(name, step), add)
                if copy is None:
                    out_ref[:, cols] = total32[:, cols].astype(out_ref.dtype)
                else:
                    total[index, :, cols] = total32[:, cols].astype(total.dtype)
            if copy is not None:
                copy.start()

        test = torus.valid(delta)
        when(test, handle)
        if copy is not None:
            later.append((test, copy.wait_send))
    for test, finish in later:
        when(test, finish)


def scatter_call(digits, axis_sizes, partial):
    orders = lines_and_pairs(digits)
    ways = [(n, s) for n, d in digits.items() for s in ((1,) if d[2] == 2 else (1, -1))]
    devices = math.prod(axis_sizes.values())
    rows, features = partial.shape[0] // devices, partial.shape[1]
    shape = Torus.__new__(Torus)
    shape.digits = digits
    count = len(shape.sites(orders[0]))
    vmem = pl.BlockSpec(memory_space=pltpu.VMEM)
    return pl.pallas_call(
        functools.partial(scatter_kernel, digits, axis_sizes, orders, ways),
        in_specs=[vmem],
        out_specs=vmem,
        out_shape=jax.ShapeDtypeStruct((rows, features), partial.dtype),
        scratch_shapes=[
            pltpu.VMEM((len(ways), devices, rows, features), partial.dtype),
            pltpu.VMEM((devices, rows, features), partial.dtype),
            pltpu.VMEM((rows, features), jnp.float32),
            pltpu.SemaphoreType.DMA((2, count)),
            pltpu.SemaphoreType.DMA((2, len(ways), devices)),
        ],
        compiler_params=pltpu.CompilerParams(collective_id=1, has_side_effects=True, vmem_limit_bytes=40 << 20),
    )(partial.reshape(devices, rows, features))


def coef_of(routes, gates):
    lanes = jnp.arange(LANES, dtype=jnp.int32)
    hit = routes[:, :, None] == lanes[None, None, :]
    coef = jnp.sum(jnp.where(hit, gates[:, :, None].astype(jnp.float32), 0.0), axis=1)
    return coef.astype(jnp.bfloat16)


def dense_per_device(digits, axis_sizes, tokens, cotangent, routes, gates, w_gate, w_up, w_down):
    gathered = gather_call(digits, axis_sizes, (tokens, cotangent, coef_of(routes, gates)))
    sel = (jnp.arange(LANES, dtype=jnp.int32) == lax.axis_index("expert")).astype(jnp.float32)[None]
    partial, grad_gate, grad_up, grad_down = main_call(sel, gathered, w_gate, w_up, w_down)
    grad_x = scatter_call(digits, axis_sizes, partial)
    return grad_x, grad_gate, grad_up, grad_down


def per_device(digits, axis_sizes, tokens, cotangent, routes, gates, w_gate, w_up, w_down):
    features = tokens.shape[1]
    rows = tokens.shape[0] * math.prod(axis_sizes.values())
    chunk = pick((256, 128), w_gate.shape[2])
    need = features * (14 * rows + 24 * chunk)
    fits = need < (56 << 20) and axis_sizes["expert"] <= LANES and features % (2 * LANES) == 0
    args = (tokens, cotangent, routes, gates, w_gate, w_up, w_down)
    return dense_per_device(digits, axis_sizes, *args) if fits else routed_per_device(*args)


def solution(mesh):
    body = functools.partial(per_device, digits_of(mesh), dict(mesh.shape))
    return jax.shard_map(
        body,
        mesh=mesh,
        in_specs=(
            P(("dp", "expert"), None),
            P(("dp", "expert"), None),
            P(("dp", "expert"), None),
            P(("dp", "expert"), None),
            P("expert", None, "dp"),
            P("expert", None, "dp"),
            P("expert", "dp", None),
        ),
        out_specs=(
            P(("dp", "expert"), None),
            P("expert", None, "dp"),
            P("expert", None, "dp"),
            P("expert", "dp", None),
        ),
        check_vma=False,
    )
```

```python
import functools
import itertools
import math

import jax
import jax.numpy as jnp
import numpy as np
from jax import lax
from jax.experimental import pallas as pl
from jax.experimental.pallas import tpu as pltpu
from jax.sharding import PartitionSpec as P


def slot_index(flat_ids, expert_count):
    onehot = (flat_ids[..., None] == jnp.arange(expert_count, dtype=jnp.int32)).astype(jnp.int32)
    return jnp.sum((jnp.cumsum(onehot, axis=-2) - onehot) * onehot, axis=-1)


def expert_terms(rows_x, rows_dy, gate_rows, gate_mat, up_mat, down_mat):
    gate_pre = jnp.dot(rows_x, gate_mat, preferred_element_type=jnp.float32)
    up_pre = jnp.dot(rows_x, up_mat, preferred_element_type=jnp.float32)
    sigmoid_g = jax.nn.sigmoid(gate_pre)
    activated = gate_pre * sigmoid_g
    gate_scale = gate_rows.astype(jnp.float32)[:, None]
    hidden = (gate_scale * activated * up_pre).astype(jnp.bfloat16)
    returned = gate_scale * jnp.dot(rows_dy, down_mat.T, preferred_element_type=jnp.float32)
    d_gate = (returned * up_pre * sigmoid_g * (1.0 + gate_pre * (1.0 - sigmoid_g))).astype(
        jnp.bfloat16
    )
    d_up = (returned * activated).astype(jnp.bfloat16)
    grad_gate = jnp.dot(rows_x.T, d_gate, preferred_element_type=jnp.float32)
    grad_up = jnp.dot(rows_x.T, d_up, preferred_element_type=jnp.float32)
    grad_down = jnp.dot(hidden.T, rows_dy, preferred_element_type=jnp.float32)
    return (d_gate, d_up, grad_gate, grad_up, grad_down)


def routed_per_device(tokens, cotangent, routes, gates, w_gate, w_up, w_down):
    tok_rows, features = tokens.shape
    top_k = routes.shape[1]
    expert_count = lax.axis_size("expert")
    capacity = min(tok_rows, (3 * tok_rows * top_k + 2 * expert_count - 1) // (2 * expert_count))
    gate_mat = w_gate[0]
    up_mat = w_up[0]
    down_mat = w_down[0]
    flat_ids = routes.reshape(-1)
    position = flat_ids * capacity + slot_index(flat_ids, expert_count)
    token_of = jnp.arange(tok_rows * top_k, dtype=jnp.int32) // top_k
    slots_all = expert_count * capacity
    send_x = jnp.zeros((slots_all, features), jnp.bfloat16).at[position].set(tokens[token_of])
    send_dy = jnp.zeros((slots_all, features), jnp.bfloat16).at[position].set(cotangent[token_of])
    send_gate = jnp.zeros((slots_all,), jnp.bfloat16).at[position].set(gates.reshape(-1))
    received = (
        lax.all_to_all(
            send_x.reshape(expert_count, capacity, features),
            "expert",
            split_axis=0,
            concat_axis=0,
            tiled=True,
        ),
        lax.all_to_all(
            send_dy.reshape(expert_count, capacity, features),
            "expert",
            split_axis=0,
            concat_axis=0,
            tiled=True,
        ),
        lax.all_to_all(
            send_gate.reshape(expert_count, capacity),
            "expert",
            split_axis=0,
            concat_axis=0,
            tiled=True,
        ),
    )
    gathered = (
        lax.all_gather(received[0], "dp", axis=0, tiled=True),
        lax.all_gather(received[1], "dp", axis=0, tiled=True),
        lax.all_gather(received[2], "dp", axis=0, tiled=True),
    )
    rows_x = gathered[0].reshape(-1, features)
    rows_dy = gathered[1].reshape(-1, features)
    d_gate, d_up, grad_gate, grad_up, grad_down = expert_terms(
        rows_x, rows_dy, gathered[2].reshape(-1), gate_mat, up_mat, down_mat
    )
    own_rows = lax.psum_scatter(
        jnp.dot(d_gate, gate_mat.T, preferred_element_type=jnp.float32)
        + jnp.dot(d_up, up_mat.T, preferred_element_type=jnp.float32),
        "dp",
        scatter_dimension=0,
        tiled=True,
    )
    returned = lax.all_to_all(
        own_rows.reshape(expert_count, capacity, features),
        "expert",
        split_axis=0,
        concat_axis=0,
        tiled=True,
    )
    selected = returned.reshape(slots_all, features)[position]
    grad_x = selected.reshape(tok_rows, top_k, features).sum(axis=1)
    return (
        grad_x.astype(jnp.bfloat16),
        grad_gate.astype(jnp.bfloat16)[None],
        grad_up.astype(jnp.bfloat16)[None],
        grad_down.astype(jnp.bfloat16)[None],
    )


LANES = 128
NT = (((1,), (1,)), ((), ()))


def pick(options, size):
    return next((o for o in options if size % o == 0), size)


def main_kernel(tile, sel_ref, x_ref, dy_ref, coef_ref, wg_ref, wu_ref, wd_ref, p_ref, gg_ref, gu_ref, gd_ref, xt_ref, acc_ref):
    step = pl.program_id(0)
    features = x_ref.shape[1]

    @pl.when(step == 0)
    def _():
        for t in range(0, features, tile):
            xt_ref[t:t + tile, :] = x_ref[:, t:t + tile].T

    c = jnp.sum(coef_ref[...].astype(jnp.float32) * sel_ref[...], axis=1, keepdims=True)
    x = x_ref[...]
    g = jnp.dot(x, wg_ref[...], preferred_element_type=jnp.float32)
    u = jnp.dot(x, wu_ref[...], preferred_element_type=jnp.float32)
    r = c * lax.dot_general(dy_ref[...], wd_ref[...], NT, preferred_element_type=jnp.float32)
    s = jax.nn.sigmoid(g)
    act = g * s
    hid_t = (c * act * u).astype(jnp.bfloat16).T
    dg = (r * u * s * (1.0 + g * (1.0 - s))).astype(jnp.bfloat16)
    du = (r * act).astype(jnp.bfloat16)

    for t in range(0, features, tile):
        cols = slice(t, t + tile)
        part = lax.dot_general(dg, wg_ref[cols, :], NT, preferred_element_type=jnp.float32)
        part += lax.dot_general(du, wu_ref[cols, :], NT, preferred_element_type=jnp.float32)

        @pl.when(step == 0)
        def _():
            acc_ref[:, cols] = part

        @pl.when(step > 0)
        def _():
            acc_ref[:, cols] += part

        gg_ref[cols, :] = jnp.dot(xt_ref[cols, :], dg, preferred_element_type=jnp.float32).astype(jnp.bfloat16)
        gu_ref[cols, :] = jnp.dot(xt_ref[cols, :], du, preferred_element_type=jnp.float32).astype(jnp.bfloat16)
        gd_ref[:, cols] = jnp.dot(hid_t, dy_ref[:, cols], preferred_element_type=jnp.float32).astype(jnp.bfloat16)

    @pl.when(step == pl.num_programs(0) - 1)
    def _():
        p_ref[...] = acc_ref[...].astype(jnp.bfloat16)


def main_call(sel, gathered, w_gate, w_up, w_down):
    _, features, hidden = w_gate.shape
    rows = gathered[0].shape[0]
    chunk = pick((512, 256, 128), hidden)
    tile = pick((1792, 512, 256, 128), features)
    whole = lambda width: pl.BlockSpec((rows, width), lambda i: (0, 0), pipeline_mode=pl.Buffered(1))
    col = pl.BlockSpec((None, features, chunk), lambda i: (0, 0, i))
    row = pl.BlockSpec((None, chunk, features), lambda i: (0, i, 0))
    bf = jnp.bfloat16
    return pl.pallas_call(
        functools.partial(main_kernel, tile),
        grid=(hidden // chunk,),
        in_specs=[
            pl.BlockSpec((1, LANES), lambda i: (0, 0)),
            whole(features), whole(features), whole(LANES),
            col, col, row,
        ],
        out_specs=[pl.BlockSpec((rows, features), lambda i: (0, 0)), col, col, row],
        out_shape=[
            jax.ShapeDtypeStruct((rows, features), bf),
            jax.ShapeDtypeStruct(w_gate.shape, bf),
            jax.ShapeDtypeStruct(w_up.shape, bf),
            jax.ShapeDtypeStruct(w_down.shape, bf),
        ],
        scratch_shapes=[pltpu.VMEM((features, rows), bf), pltpu.VMEM((rows, features), jnp.float32)],
        compiler_params=pltpu.CompilerParams(dimension_semantics=("arbitrary",), vmem_limit_bytes=60 << 20),
    )(sel, *gathered, w_gate, w_up, w_down)


def digits_of(mesh):
    digits = {}
    for number, axis in enumerate(mesh.axis_names):
        line = np.moveaxis(mesh.devices, number, 0)
        line = line.reshape(line.shape[0], -1)[:, 0]
        places = [(*d.coords, d.core_on_chip) for d in line]
        stride = 1
        while stride < len(places):
            name = next(i for i in range(4) if places[stride][i] != places[0][i])
            size = len({p[name] for p in places})
            digits[name] = (axis, stride, size)
            stride *= size
    return digits


class Torus:
    def __init__(self, digits, axis_sizes):
        self.digits, self.axis_sizes = digits, axis_sizes
        self.me = {n: (lax.axis_index(a) // s) % k for n, (a, s, k) in digits.items()}

    def at(self, delta):
        place = dict(self.me)
        for name, step in delta.items():
            size = self.digits[name][2]
            place[name] = (self.me[name] + step) % 2 if size == 2 else self.me[name] + step
        return place

    def device(self, place):
        index = {a: 0 for a in self.axis_sizes}
        for name, (axis, stride, _) in self.digits.items():
            index[axis] = index[axis] + place[name] * stride
        return index

    def linear(self, place):
        index, total = self.device(place), 0
        for axis, size in self.axis_sizes.items():
            total = total * size + index[axis]
        return total

    def steps(self, name):
        return (1,) if self.digits[name][2] == 2 else (1, -1)

    def inside(self, name, step):
        size = self.digits[name][2]
        if size == 2 or step == 0:
            return None
        return self.me[name] + step < size if step > 0 else self.me[name] + step >= 0

    def sites(self, order):
        spans = []
        for name in order:
            size = self.digits[name][2]
            spans.append(range(size) if size == 2 else range(1 - size, size))
        return [dict(zip(order, combo)) for combo in itertools.product(*spans)]

    def valid(self, delta):
        found = None
        for name, step in delta.items():
            test = self.inside(name, step)
            if test is not None:
                found = test if found is None else jnp.logical_and(found, test)
        return found

    def children(self, order, delta):
        last = max([i for i, n in enumerate(order) if delta[n]], default=-1)
        found = []
        if last >= 0 and self.digits[order[last]][2] > 2:
            found.append((order[last], -1 if delta[order[last]] > 0 else 1))
        for name in order[last + 1:]:
            found += [(name, step) for step in self.steps(name)]
        return found

    def parent(self, order, delta):
        last = max(i for i, n in enumerate(order) if delta[n])
        return order[last], 1 if delta[order[last]] > 0 else -1

    def barrier(self):
        sem = pltpu.get_barrier_semaphore()
        count = 0
        for name in self.digits:
            for step in self.steps(name):
                test = self.inside(name, step)
                target = self.device(self.at({name: step}))

                def greet(target=target):
                    pl.semaphore_signal(sem, inc=1, device_id=target, device_id_type=pl.DeviceIdType.MESH)

                when(test, greet)
                count = count + (1 if test is None else test.astype(jnp.int32))
        pl.semaphore_wait(sem, count)


def when(test, body):
    if test is None:
        body()
    else:
        pl.when(test)(body)


def distance(delta):
    return sum(abs(v) for v in delta.values())


def lines_and_pairs(digits):
    lines = [n for n in digits if digits[n][2] > 2]
    pairs = [n for n in digits if digits[n][2] == 2 and n != 3]
    core = [3] if 3 in digits else []
    return tuple(lines + pairs + core), tuple(lines + pairs[::-1] + core)


def gather_kernel(digits, axis_sizes, orders, *refs):
    parts = len(orders)
    ins, outs = refs[:parts], refs[parts:2 * parts]
    send_sem, recv_sem, local_sem = refs[2 * parts:]
    torus = Torus(digits, axis_sizes)
    rows = ins[0].shape[0]

    def block(ref, index):
        return ref.at[pl.ds(pl.multiple_of(index * rows, rows), rows)]

    mine = torus.linear(torus.me)
    own = [pltpu.make_async_copy(ins[p], block(outs[p], mine), local_sem.at[p]) for p in range(parts)]
    torus.barrier()
    plan, used = [], [0] * parts
    for p in range(parts):
        for delta in torus.sites(orders[p]):
            plan.append((distance(delta), p, delta))
    plan.sort(key=lambda entry: entry[:2])
    later = []
    for _, p, delta in plan:
        index = torus.linear(torus.at(delta))
        root = distance(delta) == 0
        copies = []
        for name, step in torus.children(orders[p], delta):
            copies.append((torus.inside(name, step), pltpu.make_async_remote_copy(
                src_ref=ins[p] if root else block(outs[p], index),
                dst_ref=block(outs[p], index),
                send_sem=send_sem.at[p, used[p]],
                recv_sem=recv_sem.at[p, index],
                device_id=torus.device(torus.at({name: step})),
                device_id_type=pl.DeviceIdType.MESH,
            )))
            used[p] += 1

        def handle(p=p, index=index, root=root, copies=copies):
            if not root:
                pltpu.make_async_copy(ins[p], block(outs[p], index), recv_sem.at[p, index]).wait()
            for test, copy in copies:
                when(test, copy.start)

        def finish(copies=copies):
            for test, copy in copies:
                when(test, copy.wait_send)

        test = torus.valid(delta)
        when(test, handle)
        later.append((test, finish))
        if root:
            own[p].start()
    for test, finish in later:
        when(test, finish)
    for copy in own:
        copy.wait()


def gather_call(digits, axis_sizes, arrays):
    first, second = lines_and_pairs(digits)
    orders = (first, second) + (first,) * (len(arrays) - 2)
    devices = math.prod(axis_sizes.values())
    count = max(count_sends(digits, order) for order in orders)
    return pl.pallas_call(
        functools.partial(gather_kernel, digits, axis_sizes, orders),
        in_specs=[pl.BlockSpec(memory_space=pl.ANY)] * len(arrays),
        out_specs=[pl.BlockSpec(memory_space=pl.ANY)] * len(arrays),
        out_shape=[jax.ShapeDtypeStruct((devices * a.shape[0], a.shape[1]), a.dtype) for a in arrays],
        scratch_shapes=[
            pltpu.SemaphoreType.DMA((len(arrays), count)),
            pltpu.SemaphoreType.DMA((len(arrays), devices)),
            pltpu.SemaphoreType.DMA((len(arrays),)),
        ],
        compiler_params=pltpu.CompilerParams(collective_id=0, has_side_effects=True),
    )(*arrays)


def count_sends(digits, order):
    shape = Torus.__new__(Torus)
    shape.digits = digits
    return sum(len(shape.children(order, delta)) for delta in shape.sites(order))


def scatter_kernel(digits, axis_sizes, orders, ways, p_hbm, out_ref, p_ref, land, total, total32, load_sem, send_sem, recv_sem):
    torus = Torus(digits, axis_sizes)
    parts = len(orders)
    width = p_hbm.shape[2] // parts
    plan = []
    for p in range(parts):
        for number, delta in enumerate(torus.sites(orders[p])):
            plan.append((len(torus.children(orders[p], delta)), -distance(delta), p, number, delta))
    plan.sort(key=lambda entry: entry[:4])
    load = pltpu.make_async_copy(p_hbm, p_ref, load_sem)
    load.start()
    torus.barrier()
    loaded = False
    later = []
    for _, _, p, number, delta in plan:
        order = orders[p]
        index = torus.linear(torus.at(delta))
        cols = slice(p * width, (p + 1) * width)
        root = distance(delta) == 0
        kids = torus.children(order, delta)
        source = total if kids else p_hbm
        if kids and not loaded:
            load.wait()
            loaded = True
        copy = None
        if not root:
            name, step = torus.parent(order, delta)
            way = ways.index((name, step if digits[name][2] == 2 else -step))
            copy = pltpu.make_async_remote_copy(
                src_ref=source.at[index, :, cols],
                dst_ref=land.at[way, index, :, cols],
                send_sem=send_sem.at[p, number],
                recv_sem=recv_sem.at[p, way, index],
                device_id=torus.device(torus.at({name: step})),
                device_id_type=pl.DeviceIdType.MESH,
            )

        def handle(p=p, index=index, cols=cols, kids=kids, copy=copy):
            if kids:
                total32[:, cols] = p_ref[index, :, cols].astype(jnp.float32)
                for name, step in kids:
                    way = ways.index((name, step))

                    def add(way=way):
                        here = land.at[way, index, :, cols]
                        pltpu.make_async_copy(here, here, recv_sem.at[p, way, index]).wait()
                        total32[:, cols] += land[way, index, :, cols].astype(jnp.float32)

                    when(torus.inside(name, step), add)
                if copy is None:
                    out_ref[:, cols] = total32[:, cols].astype(out_ref.dtype)
                else:
                    total[index, :, cols] = total32[:, cols].astype(total.dtype)
            if copy is not None:
                copy.start()

        test = torus.valid(delta)
        when(test, handle)
        if copy is not None:
            later.append((test, copy.wait_send))
    for test, finish in later:
        when(test, finish)


def scatter_call(digits, axis_sizes, partial):
    orders = lines_and_pairs(digits)
    ways = [(n, s) for n, d in digits.items() for s in ((1,) if d[2] == 2 else (1, -1))]
    devices = math.prod(axis_sizes.values())
    rows, features = partial.shape[0] // devices, partial.shape[1]
    shape = Torus.__new__(Torus)
    shape.digits = digits
    count = len(shape.sites(orders[0]))
    vmem = pl.BlockSpec(memory_space=pltpu.VMEM)
    return pl.pallas_call(
        functools.partial(scatter_kernel, digits, axis_sizes, orders, ways),
        in_specs=[pl.BlockSpec(memory_space=pl.ANY)],
        out_specs=vmem,
        out_shape=jax.ShapeDtypeStruct((rows, features), partial.dtype),
        scratch_shapes=[
            pltpu.VMEM((devices, rows, features), partial.dtype),
            pltpu.VMEM((len(ways), devices, rows, features), partial.dtype),
            pltpu.VMEM((devices, rows, features), partial.dtype),
            pltpu.VMEM((rows, features), jnp.float32),
            pltpu.SemaphoreType.DMA,
            pltpu.SemaphoreType.DMA((2, count)),
            pltpu.SemaphoreType.DMA((2, len(ways), devices)),
        ],
        compiler_params=pltpu.CompilerParams(collective_id=1, has_side_effects=True, vmem_limit_bytes=40 << 20),
    )(partial.reshape(devices, rows, features))


def coef_of(routes, gates):
    lanes = jnp.arange(LANES, dtype=jnp.int32)
    coef = jnp.zeros((routes.shape[0], LANES), gates.dtype)
    for k in range(routes.shape[1]):
        coef = jnp.where(routes[:, k:k + 1] == lanes, gates[:, k:k + 1], coef)
    return coef


def dense_per_device(digits, axis_sizes, tokens, cotangent, routes, gates, w_gate, w_up, w_down):
    gathered = gather_call(digits, axis_sizes, (tokens, cotangent, coef_of(routes, gates)))
    sel = (jnp.arange(LANES, dtype=jnp.int32) == lax.axis_index("expert")).astype(jnp.float32)[None]
    partial, grad_gate, grad_up, grad_down = main_call(sel, gathered, w_gate, w_up, w_down)
    grad_x = scatter_call(digits, axis_sizes, partial)
    return grad_x, grad_gate, grad_up, grad_down


def per_device(digits, axis_sizes, tokens, cotangent, routes, gates, w_gate, w_up, w_down):
    features = tokens.shape[1]
    rows = tokens.shape[0] * math.prod(axis_sizes.values())
    chunk = pick((512, 256, 128), w_gate.shape[2])
    need = features * (14 * rows + 24 * chunk)
    fits = need < (56 << 20) and axis_sizes["expert"] <= LANES and features % (2 * LANES) == 0
    args = (tokens, cotangent, routes, gates, w_gate, w_up, w_down)
    return dense_per_device(digits, axis_sizes, *args) if fits else routed_per_device(*args)


def solution(mesh):
    body = functools.partial(per_device, digits_of(mesh), dict(mesh.shape))
    return jax.shard_map(
        body,
        mesh=mesh,
        in_specs=(
            P(("dp", "expert"), None),
            P(("dp", "expert"), None),
            P(("dp", "expert"), None),
            P(("dp", "expert"), None),
            P("expert", None, "dp"),
            P("expert", None, "dp"),
            P("expert", "dp", None),
        ),
        out_specs=(
            P(("dp", "expert"), None),
            P("expert", None, "dp"),
            P("expert", None, "dp"),
            P("expert", "dp", None),
        ),
        check_vma=False,
    )
```
